32 devices in a mesh: occ: 8 (over z, x), aux: 4 (over y, core).
Axes of the slice: x: 2, y: 2, z: 4, core: 2. Of those that a mesh axis runs over, the one named last changes fastest.
Arguments:
- int_tiles: bfloat16 [32, 64, 128, 256], P('occ', 'aux'), may hold values from -0.5 to 0.5
- tile_ids: int32 [32, 64], P('occ', 'aux'), may hold values from 0 to 79, as said below
- tile_counts: int32 [32, 4], P('occ', 'aux'), may hold values from 8 to 16, as said below
- pair_list: int32 [64, 2], P('occ'), may hold values from 0 to 3
- occ_energy: float32 [32], replicated, may hold values from -2 to -0.5
- vir_energy: float32 [256], replicated, may hold values from 0.2 to 3
Outputs:
- gamma_tiles: bfloat16 [32, 64, 128, 256], P('occ', 'aux')
- density: float32 [256, 256], P('aux')
The draws below stay inside these ranges and needn't reach their ends.
Inputs may be any that keep to these rules, and one draw needn't show every extreme that they name: `tile_ids`: within one orbital and one aux index's share the 16 tile numbers are distinct. Only the first tile_counts slots of a share are live; tiles and numbers of the others are never read. `pair_list`: column 0 indexes the asking occ index's orbitals, column 1 those of occ index r.
All inputs are finite; a program needn't handle non-finite values.
Results may differ from the reference program's by a relative error of at most 0.0085.
Values may be sent and summed in bfloat16 or wider, within the bound.
A program may use at most 256 MiB of HBM per device.

```python
import math
import jax
import jax.numpy as jnp
from jax import lax

TILE = 128
NV = 256
AUXT_DEV = 80
SLOTS = 16
O_DEV = 4
CAP = 1
NOCC = 32
NPAIR = 64
N_OCC = 8
N_AUX = 4


def draw_tile_ids(key, part):
    common_key = jax.random.fold_in(key, 11)
    jitter_key = jax.random.fold_in(key, 23)
    tile_range = jnp.arange(AUXT_DEV, dtype=jnp.int32)
    common = jax.random.randint(common_key, (N_AUX, AUXT_DEV), 0, 1048576) * AUXT_DEV + tile_range
    common_order = jnp.argsort(common, axis=-1, stable=True).astype(jnp.int32)
    common_rank = jnp.argsort(common_order, axis=-1, stable=True).astype(jnp.int32)
    jitter = jax.random.randint(jitter_key, (NOCC, N_AUX, AUXT_DEV), 0, 24)
    scores = (common_rank[None, :, :] * 8 + jitter) * AUXT_DEV + tile_range
    scores = scores.at[0, 0, AUXT_DEV - 1].set(-1)
    ordering = jnp.argsort(scores, axis=-1, stable=True).astype(jnp.int32)
    return ordering[:, :, :SLOTS].reshape(NOCC, N_AUX * SLOTS)


def draw_tile_counts(key, part):
    lowest = max(1, SLOTS // 2)
    counts = jax.random.randint(key, (NOCC, N_AUX), lowest, SLOTS + 1)
    counts = counts.at[0].set(SLOTS)
    counts = counts.at[1, 0].set(lowest)
    return counts.astype(jnp.int32)


def set_ends(array, key, smallest, high):
    shape = array.shape
    index_at = [jax.random.randint(jax.random.fold_in(key, axis), (), 0, shape[axis]) for axis in range(len(shape))]
    array = array.at[tuple(index_at)].set(smallest)
    longest = shape.index(max(shape))
    index_at[longest] = (index_at[longest] + 1) % shape[longest]
    return array.at[tuple(index_at)].set(high)


def block_scale(rng, extent, shards, low, top_value):
    factor_of, own = 1.0, jax.random.fold_in(rng, 6)
    for dim, shards_of in shards:
        draws = jnp.exp(jax.random.uniform(jax.random.fold_in(own, dim), (shards_of,), jnp.float32, low / len(shards), top_value / len(shards)))
        factor_of = factor_of * jnp.repeat(draws, extent[dim] // shards_of).reshape([-1 if axis == dim else 1 for axis in range(len(extent))])
    return factor_of


def scatter_about(rng, extent, deviation, most, pieces=(), kind=jnp.bfloat16):
    result = deviation * jax.random.normal(rng, extent, jnp.float32)
    if pieces:
        result = result * block_scale(rng, extent, pieces, -0.22, 0.18)
    return jnp.clip(result, -most, most).astype(kind)


def setup_inputs(seed: int = 0) -> dict:
    key_of = jax.random.split(jax.random.key(seed), 7)
    int_tiles = scatter_about(key_of[0], (NOCC, N_AUX * SLOTS, TILE, NV), 0.08, 0.5, ((0, 8), (1, 4)))
    tile_ids = draw_tile_ids(jax.random.fold_in(key_of[6], 71), 0)
    tile_counts = draw_tile_counts(jax.random.fold_in(key_of[6], 71), 0)
    pair_list = set_ends(jax.random.randint(key_of[3], (NPAIR, 2), 0, O_DEV), jax.random.fold_in(key_of[3], 1), 0, O_DEV - 1).astype(jnp.int32)
    occ_energy = jnp.clip(jax.random.uniform(key_of[4], (NOCC,), jnp.float32, -2.0, -0.5), -2.0, -0.5)
    vir_energy = jnp.clip(jnp.exp(jax.random.uniform(key_of[5], (NV,), jnp.float32, math.log(0.2), math.log(3.0))), 0.2, 3.0)
    return {"int_tiles": int_tiles, "tile_ids": tile_ids, "tile_counts": tile_counts, "pair_list": pair_list, "occ_energy": occ_energy, "vir_energy": vir_energy}


def expand(tile_block, tile_numbers, counts):
    slot_index = jnp.arange(N_AUX * SLOTS, dtype=jnp.int32)
    share_index = slot_index // SLOTS
    live_slot = (slot_index - share_index * SLOTS) < counts[share_index]
    tile_place = (share_index * AUXT_DEV + tile_numbers).astype(jnp.int32)
    kept_tiles = jnp.where(live_slot[:, None, None], tile_block, jnp.zeros_like(tile_block))
    dense_tiles = jnp.zeros((N_AUX * AUXT_DEV, TILE, NV), tile_block.dtype).at[tile_place].add(kept_tiles)
    return kept_tiles, dense_tiles, tile_place, live_slot


def reference(int_tiles, tile_ids, tile_counts, pair_list, occ_energy, vir_energy):
    pair_dev = N_OCC * CAP
    pair_rows = jnp.arange(N_OCC * pair_dev, dtype=jnp.int32)
    first_orb = (pair_rows // pair_dev) * O_DEV + pair_list[:, 0]
    second_orb = ((pair_rows % pair_dev) // CAP) * O_DEV + pair_list[:, 1]

    def one_pair(running, pair_index):
        gamma_sum, density = running
        left_orb = first_orb[pair_index]
        right_orb = second_orb[pair_index]
        kept_left, dense_left, place_left, live_left = expand(int_tiles[left_orb], tile_ids[left_orb], tile_counts[left_orb])
        kept_right, dense_right, place_right, live_right = expand(int_tiles[right_orb], tile_ids[right_orb], tile_counts[right_orb])
        zero_rows = jnp.zeros_like(kept_left)
        rows_right = jnp.where(live_left[:, None, None], dense_right[place_left], zero_rows)
        rows_left = jnp.where(live_right[:, None, None], dense_left[place_right], zero_rows)
        coulomb = lax.dot_general(kept_left.reshape(-1, NV), rows_right.reshape(-1, NV), (((0,), (0,)), ((), ())), preferred_element_type=jnp.float32)
        denominator = occ_energy[left_orb] + occ_energy[right_orb] - vir_energy[:, None] - vir_energy[None, :]
        amplitude = coulomb / denominator
        spin_mixed = 2.0 * amplitude - amplitude.T
        density = density + jnp.dot(amplitude, spin_mixed.T, precision=lax.Precision.HIGHEST) + jnp.dot(amplitude.T, spin_mixed, precision=lax.Precision.HIGHEST)
        weights = spin_mixed.astype(jnp.bfloat16)
        part_left = lax.dot_general(rows_right.reshape(-1, NV), weights, (((1,), (1,)), ((), ())), preferred_element_type=jnp.float32)
        part_right = jnp.dot(rows_left.reshape(-1, NV), weights, preferred_element_type=jnp.float32)
        part_left = lax.optimization_barrier(part_left.astype(jnp.bfloat16)).astype(jnp.float32)
        part_right = lax.optimization_barrier(part_right.astype(jnp.bfloat16)).astype(jnp.float32)
        gamma_sum = gamma_sum.at[left_orb].add(part_left.reshape(N_AUX * SLOTS, TILE, NV))
        gamma_sum = gamma_sum.at[right_orb].add(part_right.reshape(N_AUX * SLOTS, TILE, NV))
        return (gamma_sum, density), None

    start_gamma = jnp.zeros((NOCC, N_AUX * SLOTS, TILE, NV), jnp.float32)
    start_density = jnp.zeros((NV, NV), jnp.float32)
    (gamma_sum, density), unused = lax.scan(one_pair, (start_gamma, start_density), pair_rows)
    return gamma_sum.astype(jnp.bfloat16), density
```

```python
import jax
import jax.numpy as jnp
from jax import lax
from jax.experimental import pallas as pl
from jax.experimental.pallas import tpu as pltpu
from jax.sharding import PartitionSpec as P

CHUNK_TILES = 4


def slot_match(wanted_ids, source_ids):
    same = (wanted_ids[:, :, None] == source_ids[:, None, :]) & (wanted_ids[:, :, None] >= 0)
    slots = jnp.arange(source_ids.shape[1], dtype=jnp.int32)
    return jnp.max(jnp.where(same, slots[None, None, :], -1), axis=2).astype(jnp.int32)


def gather_tiles(match_ref, row, source_ref, rows_ref):
    slot_count = source_ref.shape[1]
    for slot in range(slot_count):
        found = match_ref[row, slot]

        @pl.when(found >= 0)
        def _():
            rows_ref[slot] = source_ref[0, found]

        @pl.when(found < 0)
        def _():
            rows_ref[slot] = jnp.zeros(rows_ref.shape[1:], rows_ref.dtype)


def coulomb_kernel(orb_ref, match_ref, left_ref, right_ref, out_ref, rows_ref, total_ref):
    pair = pl.program_id(0)
    slot_count, tile_rows, width = rows_ref.shape
    gather_tiles(match_ref, pair, right_ref, rows_ref)
    total_ref[...] = jnp.zeros_like(total_ref)
    chunk = min(CHUNK_TILES, slot_count)

    @pl.loop(0, slot_count // chunk)
    def _(step):
        first = step * chunk
        left = left_ref[0, pl.ds(first, chunk)].reshape(chunk * tile_rows, width)
        right = rows_ref[pl.ds(first, chunk)].reshape(chunk * tile_rows, width)
        total_ref[...] += lax.dot_general(
            left, right, (((0,), (0,)), ((), ())), preferred_element_type=jnp.float32
        )

    out_ref[0] = total_ref[...].astype(out_ref.dtype)


def coulomb_call(orbitals, match, left, own):
    pair_count, slot_count, tile_rows, width = left.shape
    block = (1, slot_count, tile_rows, width)
    return pl.pallas_call(
        coulomb_kernel,
        grid_spec=pltpu.PrefetchScalarGridSpec(
            num_scalar_prefetch=2,
            grid=(pair_count,),
            in_specs=[
                pl.BlockSpec(block, lambda p, orb, m: (p, 0, 0, 0)),
                pl.BlockSpec(block, lambda p, orb, m: (orb[p], 0, 0, 0)),
            ],
            out_specs=pl.BlockSpec((1, width, width), lambda p, orb, m: (p, 0, 0)),
            scratch_shapes=[
                pltpu.VMEM((slot_count, tile_rows, width), left.dtype),
                pltpu.VMEM((width, width), jnp.float32),
            ],
        ),
        out_shape=jax.ShapeDtypeStruct((pair_count, width, width), jnp.bfloat16),
        compiler_params=pltpu.CompilerParams(vmem_limit_bytes=32 << 20),
        cost_estimate=pl.CostEstimate(
            flops=2 * pair_count * slot_count * tile_rows * width * width,
            bytes_accessed=4 * pair_count * slot_count * tile_rows * width,
            transcendentals=0,
        ),
    )(orbitals, match, left, own)


def add_terms(transposed, orb_ref, match_ref, source_ref, weight_ref, total_ref, rows_ref):
    term = pl.program_id(0)
    slot_count, tile_rows, width = rows_ref.shape
    gather_tiles(match_ref, term, source_ref, rows_ref)
    chunk = min(CHUNK_TILES, slot_count)
    orb = orb_ref[term]

    @pl.loop(0, slot_count // chunk)
    def _(step):
        first = step * chunk
        rows = rows_ref[pl.ds(first, chunk)].reshape(chunk * tile_rows, width)
        product = lax.dot_general(
            rows,
            weight_ref[0],
            (((1,), (1 if transposed else 0,)), ((), ())),
            preferred_element_type=jnp.float32,
        )
        total_ref[orb, pl.ds(first, chunk)] += product.reshape(chunk, tile_rows, width)


def first_gamma_kernel(orb_ref, match_ref, source_ref, weight_ref, total_ref, rows_ref):
    @pl.when(pl.program_id(0) == 0)
    def _():
        total_ref[...] = jnp.zeros_like(total_ref)

    add_terms(False, orb_ref, match_ref, source_ref, weight_ref, total_ref, rows_ref)


def last_gamma_kernel(
    orb_ref, match_ref, source_ref, weight_ref, start_ref, out_ref, rows_ref, total_ref
):
    @pl.when(pl.program_id(0) == 0)
    def _():
        total_ref[...] = start_ref[...]

    add_terms(True, orb_ref, match_ref, source_ref, weight_ref, total_ref, rows_ref)

    @pl.when(pl.program_id(0) == pl.num_programs(0) - 1)
    def _():
        out_ref[...] = total_ref[...].astype(out_ref.dtype)


def gamma_call(orbitals, match, source, weights, start, orb_count):
    term_count, slot_count, tile_rows, width = source.shape
    total_shape = (orb_count, slot_count, tile_rows, width)
    whole = pl.BlockSpec(
        total_shape, lambda t, orb, m: (0, 0, 0, 0), pipeline_mode=pl.Buffered(1)
    )
    in_specs = [
        pl.BlockSpec((1, slot_count, tile_rows, width), lambda t, orb, m: (t, 0, 0, 0)),
        pl.BlockSpec((1, width, width), lambda t, orb, m: (t, 0, 0)),
    ]
    scratch = [pltpu.VMEM((slot_count, tile_rows, width), source.dtype)]
    operands = [orbitals, match, source, weights]
    if start is None:
        body, out_type = first_gamma_kernel, jnp.float32
    else:
        body, out_type = last_gamma_kernel, jnp.bfloat16
        in_specs.append(whole)
        scratch.append(pltpu.VMEM(total_shape, jnp.float32))
        operands.append(start)
    return pl.pallas_call(
        body,
        grid_spec=pltpu.PrefetchScalarGridSpec(
            num_scalar_prefetch=2,
            grid=(term_count,),
            in_specs=in_specs,
            out_specs=whole,
            scratch_shapes=scratch,
        ),
        out_shape=jax.ShapeDtypeStruct(total_shape, out_type),
        compiler_params=pltpu.CompilerParams(vmem_limit_bytes=48 << 20),
        cost_estimate=pl.CostEstimate(
            flops=2 * term_count * slot_count * tile_rows * width * width,
            bytes_accessed=2 * term_count * slot_count * tile_rows * width
            + 8 * orb_count * slot_count * tile_rows * width,
            transcendentals=0,
        ),
    )(*operands)


def exchange(blocks, axis):
    return lax.all_to_all(blocks, axis, split_axis=0, concat_axis=0, tiled=True)


def per_device(int_tiles, tile_ids, tile_counts, pair_list, occ_energy, vir_energy):
    peer_count = lax.axis_size("occ")
    group_count = lax.axis_size("aux")
    orb_count, slot_count, tile_rows, width = int_tiles.shape
    pair_count = pair_list.shape[0]
    per_peer = pair_count // peer_count
    me = lax.axis_index("occ")
    share = lax.axis_index("aux")

    here_index = pair_list[:, 0]
    left = exchange(int_tiles[here_index], "occ")

    slot_range = jnp.arange(slot_count, dtype=jnp.int32)
    live_ids = jnp.where(slot_range[None, :] < tile_counts, tile_ids, -1)
    packed = jnp.concatenate([pair_list.reshape(-1), live_ids.reshape(-1)])
    everyone = lax.all_gather(packed, "occ")
    all_pairs = everyone[:, : 2 * pair_count].reshape(peer_count, peer_count, per_peer, 2)
    all_ids = everyone[:, 2 * pair_count :].reshape(peer_count * orb_count, slot_count)
    asked = lax.dynamic_index_in_dim(all_pairs, me, 1, keepdims=False).reshape(pair_count, 2)
    source = jnp.arange(pair_count, dtype=jnp.int32) // per_peer
    left_global = source * orb_count + asked[:, 0]
    asked_for = asked[:, 1]
    left_ids = all_ids[left_global]
    right_ids = all_ids[source * orb_count + pair_list[:, 1]]
    asked_ids = live_ids[asked_for]
    coulomb_match = slot_match(left_ids, asked_ids)
    asked_match = slot_match(asked_ids, left_ids)
    here_match = slot_match(live_ids[here_index], right_ids)

    left, to_askers = lax.optimization_barrier((left, int_tiles[asked_for]))
    right = exchange(to_askers, "occ")

    partial = coulomb_call(asked_for, coulomb_match, left, int_tiles)
    share_pairs = pair_count // group_count
    parts = exchange(partial, "aux").reshape(group_count, share_pairs, width, width)
    coulomb = jnp.sum(parts.astype(jnp.float32), axis=0)
    energy_pair = occ_energy[left_global] + occ_energy[me * orb_count + asked_for]
    energy_pair = lax.dynamic_slice_in_dim(energy_pair, share * share_pairs, share_pairs, 0)
    denominator = energy_pair[:, None, None] - vir_energy[None, :, None] - vir_energy[None, None, :]
    amplitude = coulomb / denominator
    mixed = 2.0 * amplitude - jnp.swapaxes(amplitude, 1, 2)
    share_weights = mixed.astype(jnp.bfloat16)

    weights = lax.all_gather(share_weights, "aux", axis=0, tiled=True)
    row_block = width // group_count
    weight_rows = lax.dynamic_slice_in_dim(weights, share * row_block, row_block, 1)
    here_weights = lax.all_gather(exchange(weight_rows, "occ"), "aux", axis=1, tiled=True)

    density = jnp.einsum(
        "rac,rbc->ab", amplitude, mixed, precision=lax.Precision.HIGHEST
    ) + jnp.einsum("rca,rcb->ab", amplitude, mixed, precision=lax.Precision.HIGHEST)
    density = exchange(density.astype(jnp.bfloat16), "aux").reshape(group_count, row_block, width)
    density = jnp.sum(density.astype(jnp.float32), axis=0).astype(jnp.bfloat16)
    density = jnp.sum(lax.all_gather(density, "occ").astype(jnp.float32), axis=0)

    start = gamma_call(asked_for, asked_match, left, weights, None, orb_count)
    gamma = gamma_call(here_index, here_match, right, here_weights, start, orb_count)
    return gamma, density


def solution(mesh):
    placed = (
        P("occ", "aux", None, None),
        P("occ", "aux"),
        P("occ", "aux"),
        P("occ", None),
        P(),
        P(),
    )
    return jax.shard_map(
        per_device,
        mesh=mesh,
        in_specs=placed,
        out_specs=(P("occ", "aux", None, None), P("aux", None)),
        check_vma=False,
    )
```

```python
import jax
import jax.numpy as jnp
from jax import lax
from jax.experimental import pallas as pl
from jax.experimental.pallas import tpu as pltpu
from jax.sharding import PartitionSpec as P

CHUNK_TILES = 4


def slot_match(wanted_ids, source_ids):
    same = (wanted_ids[:, :, None] == source_ids[:, None, :]) & (wanted_ids[:, :, None] >= 0)
    slots = jnp.arange(source_ids.shape[1], dtype=jnp.int32)
    return jnp.max(jnp.where(same, slots[None, None, :], -1), axis=2).astype(jnp.int32)


def gather_tiles(match_ref, row, source_ref, rows_ref):
    slot_count = source_ref.shape[1]
    for slot in range(slot_count):
        found = match_ref[row, slot]

        @pl.when(found >= 0)
        def _():
            rows_ref[slot] = source_ref[0, found]

        @pl.when(found < 0)
        def _():
            rows_ref[slot] = jnp.zeros(rows_ref.shape[1:], rows_ref.dtype)


def coulomb_kernel(orb_ref, match_ref, left_ref, right_ref, out_ref, rows_ref, total_ref):
    pair = pl.program_id(0)
    slot_count, tile_rows, width = rows_ref.shape
    gather_tiles(match_ref, pair, right_ref, rows_ref)
    total_ref[...] = jnp.zeros_like(total_ref)
    chunk = min(CHUNK_TILES, slot_count)

    @pl.loop(0, slot_count // chunk)
    def _(step):
        first = step * chunk
        left = left_ref[0, pl.ds(first, chunk)].reshape(chunk * tile_rows, width)
        right = rows_ref[pl.ds(first, chunk)].reshape(chunk * tile_rows, width)
        total_ref[...] += lax.dot_general(
            left, right, (((0,), (0,)), ((), ())), preferred_element_type=jnp.float32
        )

    out_ref[0] = total_ref[...].astype(out_ref.dtype)


def coulomb_call(orbitals, match, left, own):
    pair_count, slot_count, tile_rows, width = left.shape
    block = (1, slot_count, tile_rows, width)
    return pl.pallas_call(
        coulomb_kernel,
        grid_spec=pltpu.PrefetchScalarGridSpec(
            num_scalar_prefetch=2,
            grid=(pair_count,),
            in_specs=[
                pl.BlockSpec(block, lambda p, orb, m: (p, 0, 0, 0)),
                pl.BlockSpec(block, lambda p, orb, m: (orb[p], 0, 0, 0)),
            ],
            out_specs=pl.BlockSpec((1, width, width), lambda p, orb, m: (p, 0, 0)),
            scratch_shapes=[
                pltpu.VMEM((slot_count, tile_rows, width), left.dtype),
                pltpu.VMEM((width, width), jnp.float32),
            ],
        ),
        out_shape=jax.ShapeDtypeStruct((pair_count, width, width), jnp.bfloat16),
        compiler_params=pltpu.CompilerParams(vmem_limit_bytes=32 << 20),
        cost_estimate=pl.CostEstimate(
            flops=2 * pair_count * slot_count * tile_rows * width * width,
            bytes_accessed=4 * pair_count * slot_count * tile_rows * width,
            transcendentals=0,
        ),
    )(orbitals, match, left, own)


def add_terms(orb_ref, match_ref, source_ref, weight_ref, total_ref, rows_ref):
    term = pl.program_id(0)
    slot_count, tile_rows, width = rows_ref.shape
    gather_tiles(match_ref, term, source_ref, rows_ref)
    chunk = min(CHUNK_TILES, slot_count)
    orb = orb_ref[term]

    @pl.loop(0, slot_count // chunk)
    def _(step):
        first = step * chunk
        rows = rows_ref[pl.ds(first, chunk)].reshape(chunk * tile_rows, width)
        product = lax.dot_general(
            rows,
            weight_ref[0],
            (((1,), (0,)), ((), ())),
            preferred_element_type=jnp.float32,
        )
        total_ref[orb, pl.ds(first, chunk)] += product.reshape(chunk, tile_rows, width)


def first_gamma_kernel(orb_ref, match_ref, source_ref, weight_ref, total_ref, rows_ref):
    @pl.when(pl.program_id(0) == 0)
    def _():
        total_ref[...] = jnp.zeros_like(total_ref)

    add_terms(orb_ref, match_ref, source_ref, weight_ref, total_ref, rows_ref)


def last_gamma_kernel(
    orb_ref, match_ref, source_ref, weight_ref, start_ref, out_ref, rows_ref, total_ref
):
    @pl.when(pl.program_id(0) == 0)
    def _():
        total_ref[...] = start_ref[...]

    add_terms(orb_ref, match_ref, source_ref, weight_ref, total_ref, rows_ref)

    @pl.when(pl.program_id(0) == pl.num_programs(0) - 1)
    def _():
        out_ref[...] = total_ref[...].astype(out_ref.dtype)


def gamma_call(orbitals, match, source, weights, start, orb_count):
    term_count, slot_count, tile_rows, width = source.shape
    total_shape = (orb_count, slot_count, tile_rows, width)
    whole = pl.BlockSpec(
        total_shape, lambda t, orb, m: (0, 0, 0, 0), pipeline_mode=pl.Buffered(1)
    )
    in_specs = [
        pl.BlockSpec((1, slot_count, tile_rows, width), lambda t, orb, m: (t, 0, 0, 0)),
        pl.BlockSpec((1, width, width), lambda t, orb, m: (t, 0, 0)),
    ]
    scratch = [pltpu.VMEM((slot_count, tile_rows, width), source.dtype)]
    operands = [orbitals, match, source, weights]
    if start is None:
        body, out_type = first_gamma_kernel, jnp.float32
    else:
        body, out_type = last_gamma_kernel, jnp.bfloat16
        in_specs.append(whole)
        scratch.append(pltpu.VMEM(total_shape, jnp.float32))
        operands.append(start)
    return pl.pallas_call(
        body,
        grid_spec=pltpu.PrefetchScalarGridSpec(
            num_scalar_prefetch=2,
            grid=(term_count,),
            in_specs=in_specs,
            out_specs=whole,
            scratch_shapes=scratch,
        ),
        out_shape=jax.ShapeDtypeStruct(total_shape, out_type),
        compiler_params=pltpu.CompilerParams(vmem_limit_bytes=48 << 20),
        cost_estimate=pl.CostEstimate(
            flops=2 * term_count * slot_count * tile_rows * width * width,
            bytes_accessed=2 * term_count * slot_count * tile_rows * width
            + 8 * orb_count * slot_count * tile_rows * width,
            transcendentals=0,
        ),
    )(*operands)


def exchange(blocks, axis):
    count = lax.axis_size(axis)
    me = lax.axis_index(axis)
    arrived = [lax.dynamic_index_in_dim(blocks, me, 0, keepdims=False)]
    for shift in range(1, count):
        block = lax.dynamic_index_in_dim(blocks, lax.rem(me + shift, count), 0, keepdims=False)
        arrived.append(lax.ppermute(block, axis, [(d, (d + shift) % count) for d in range(count)]))
    return arrived


def sum_everywhere(block, axis):
    count = lax.axis_size(axis)
    total = block.astype(jnp.float32)
    for shift in range(1, count):
        moved = lax.ppermute(block, axis, [(d, (d + shift) % count) for d in range(count)])
        total = total + moved.astype(jnp.float32)
    return total


def pair_weights(partial, energy_pair, vir_energy):
    group_count = lax.axis_size("aux")
    share = lax.axis_index("aux")
    term_count, width = partial.shape[:2]
    share_terms = term_count // group_count
    parts = exchange(partial.reshape(group_count, share_terms, width, width), "aux")
    coulomb = parts[0].astype(jnp.float32)
    for part in parts[1:]:
        coulomb = coulomb + part.astype(jnp.float32)
    energy = lax.dynamic_slice_in_dim(energy_pair, share * share_terms, share_terms, 0)
    denominator = energy[:, None, None] - vir_energy[None, :, None] - vir_energy[None, None, :]
    amplitude = coulomb / denominator
    mixed = 2.0 * amplitude - jnp.swapaxes(amplitude, 1, 2)
    weights = lax.all_gather(mixed.astype(jnp.bfloat16), "aux", axis=0, tiled=True)
    amplitude, mixed = amplitude[0::2], mixed[0::2]
    density = jnp.einsum(
        "rac,rbc->ab", amplitude, mixed, precision=lax.Precision.HIGHEST
    ) + jnp.einsum("rca,rcb->ab", amplitude, mixed, precision=lax.Precision.HIGHEST)
    return weights, density


def per_device(int_tiles, tile_ids, tile_counts, pair_list, occ_energy, vir_energy):
    peer_count = lax.axis_size("occ")
    group_count = lax.axis_size("aux")
    orb_count, slot_count, tile_rows, width = int_tiles.shape
    assert pair_list.shape[0] == peer_count and peer_count % 2 == 0
    half = peer_count // 2
    assert (2 * half) % (2 * group_count) == 0
    me = lax.axis_index("occ")

    slot_range = jnp.arange(slot_count, dtype=jnp.int32)
    live_ids = jnp.where(slot_range[None, :] < tile_counts, tile_ids, -1)
    packed = jnp.concatenate([pair_list.reshape(-1), live_ids.reshape(-1)])
    everyone = lax.all_gather(packed, "occ")
    everyone, own_tiles = lax.optimization_barrier((everyone, int_tiles))
    all_pairs = everyone[:, : 2 * peer_count].reshape(peer_count, peer_count, 2)
    all_ids = everyone[:, 2 * peer_count :].reshape(peer_count * orb_count, slot_count)

    near = me // half * half + jnp.arange(half, dtype=jnp.int32)
    far = lax.rem(near + half, peer_count)
    partner = lax.rem(me + half, peer_count)

    def wanted_of(owner):
        return jnp.stack([all_pairs[owner, near, 0], all_pairs[near, owner, 1]], axis=1).reshape(-1)

    def terms_of(peers):
        remote = jnp.stack([all_pairs[peers, me, 0], all_pairs[me, peers, 1]], axis=1)
        own = jnp.stack([all_pairs[peers, me, 1], all_pairs[me, peers, 0]], axis=1).reshape(-1)
        remote = (peers[:, None] * orb_count + remote).reshape(-1)
        remote_ids, own_ids = all_ids[remote], live_ids[own]
        energy_pair = occ_energy[remote] + occ_energy[me * orb_count + own]
        return (
            own,
            slot_match(remote_ids, own_ids),
            slot_match(own_ids, remote_ids),
            energy_pair,
        )

    groups = [list(range(half)), list(range(half, peer_count))]

    def near_exchange(tiles, owner):
        return lax.all_to_all(
            tiles[wanted_of(owner)],
            "occ",
            split_axis=0,
            concat_axis=0,
            axis_index_groups=groups,
            tiled=True,
        )

    swapped = [(d, (d + half) % peer_count) for d in range(peer_count)]
    partner_tiles = lax.ppermute(own_tiles, "occ", swapped)
    near_tiles = near_exchange(own_tiles, me)
    far_tiles = near_exchange(partner_tiles, partner)

    own, coulomb_match, near_match, energy_pair = terms_of(near)
    partial = coulomb_call(own, coulomb_match, near_tiles, int_tiles)
    weights, density = pair_weights(partial, energy_pair, vir_energy)
    gamma = gamma_call(own, near_match, near_tiles, weights, None, orb_count)

    far_tiles, gamma = lax.optimization_barrier((far_tiles, gamma))
    own, coulomb_match, far_match, energy_pair = terms_of(far)
    partial = coulomb_call(own, coulomb_match, far_tiles, int_tiles)
    weights, more_density = pair_weights(partial, energy_pair, vir_energy)

    density = (density + more_density).astype(jnp.bfloat16)
    parts = exchange(density.reshape(group_count, width // group_count, width), "aux")
    density = parts[0].astype(jnp.float32)
    for part in parts[1:]:
        density = density + part.astype(jnp.float32)
    density = sum_everywhere(density.astype(jnp.bfloat16), "occ")

    gamma = gamma_call(own, far_match, far_tiles, weights, gamma, orb_count)
    return gamma, density


def solution(mesh):
    placed = (
        P("occ", "aux", None, None),
        P("occ", "aux"),
        P("occ", "aux"),
        P("occ", None),
        P(),
        P(),
    )
    return jax.shard_map(
        per_device,
        mesh=mesh,
        in_specs=placed,
        out_specs=(P("occ", "aux", None, None), P("aux", None)),
        check_vma=False,
    )
```

```python
import jax
import jax.numpy as jnp
from jax import lax
from jax.experimental import pallas as pl
from jax.experimental.pallas import tpu as pltpu
from jax.sharding import PartitionSpec as P

CHUNK_TILES = 4


def slot_match(wanted_ids, source_ids):
    same = (wanted_ids[:, :, None] == source_ids[:, None, :]) & (wanted_ids[:, :, None] >= 0)
    slots = jnp.arange(source_ids.shape[1], dtype=jnp.int32)
    return jnp.max(jnp.where(same, slots[None, None, :], -1), axis=2).astype(jnp.int32)


def gather_tiles(match_ref, row, source_ref, rows_ref):
    slot_count = source_ref.shape[1]
    for slot in range(slot_count):
        found = match_ref[row, slot]

        @pl.when(found >= 0)
        def _():
            rows_ref[slot] = source_ref[0, found]

        @pl.when(found < 0)
        def _():
            rows_ref[slot] = jnp.zeros(rows_ref.shape[1:], rows_ref.dtype)


def coulomb_kernel(orb_ref, match_ref, remote_ref, flipped_ref, out_ref, rows_ref):
    slot_count, tile_rows, width = rows_ref.shape
    gather_tiles(match_ref, pl.program_id(0), remote_ref, rows_ref)
    out_ref[0] = jnp.dot(
        flipped_ref[0],
        rows_ref[...].reshape(slot_count * tile_rows, width),
        preferred_element_type=jnp.float32,
    ).astype(out_ref.dtype)


def coulomb_call(orbitals, match, remote, flipped):
    term_count, slot_count, tile_rows, width = remote.shape
    return pl.pallas_call(
        coulomb_kernel,
        grid_spec=pltpu.PrefetchScalarGridSpec(
            num_scalar_prefetch=2,
            grid=(term_count,),
            in_specs=[
                pl.BlockSpec((1, slot_count, tile_rows, width), lambda t, orb, m: (t, 0, 0, 0)),
                pl.BlockSpec((1, width, slot_count * tile_rows), lambda t, orb, m: (orb[t], 0, 0)),
            ],
            out_specs=pl.BlockSpec((1, width, width), lambda t, orb, m: (t, 0, 0)),
            scratch_shapes=[pltpu.VMEM((slot_count, tile_rows, width), remote.dtype)],
        ),
        out_shape=jax.ShapeDtypeStruct((term_count, width, width), jnp.bfloat16),
        compiler_params=pltpu.CompilerParams(vmem_limit_bytes=56 << 20),
        cost_estimate=pl.CostEstimate(
            flops=2 * term_count * slot_count * tile_rows * width * width,
            bytes_accessed=4 * term_count * slot_count * tile_rows * width,
            transcendentals=0,
        ),
    )(orbitals, match, remote, flipped)


def add_terms(orb_ref, match_ref, source_ref, weight_ref, total_ref, rows_ref):
    term = pl.program_id(0)
    slot_count, tile_rows, width = rows_ref.shape
    gather_tiles(match_ref, term, source_ref, rows_ref)
    chunk = min(CHUNK_TILES, slot_count)
    orb = orb_ref[term]

    @pl.loop(0, slot_count // chunk)
    def _(step):
        first = step * chunk
        rows = rows_ref[pl.ds(first, chunk)].reshape(chunk * tile_rows, width)
        product = lax.dot_general(
            rows,
            weight_ref[0],
            (((1,), (1,)), ((), ())),
            preferred_element_type=jnp.float32,
        )
        total_ref[orb, pl.ds(first, chunk)] += product.reshape(chunk, tile_rows, width)


def first_gamma_kernel(orb_ref, match_ref, source_ref, weight_ref, total_ref, rows_ref):
    @pl.when(pl.program_id(0) == 0)
    def _():
        total_ref[...] = jnp.zeros_like(total_ref)

    add_terms(orb_ref, match_ref, source_ref, weight_ref, total_ref, rows_ref)


def next_gamma_kernel(
    orb_ref, match_ref, source_ref, weight_ref, start_ref, out_ref, rows_ref, total_ref, sem
):
    @pl.when(pl.program_id(0) == 0)
    def _():
        load = pltpu.make_async_copy(start_ref, total_ref, sem)
        load.start()
        load.wait()

    add_terms(orb_ref, match_ref, source_ref, weight_ref, total_ref, rows_ref)

    @pl.when(pl.program_id(0) == pl.num_programs(0) - 1)
    def _():
        out_ref[...] = total_ref[...].astype(out_ref.dtype)


def gamma_call(orbitals, match, source, weights, start, orb_count, out_type):
    term_count, slot_count, tile_rows, width = source.shape
    total_shape = (orb_count, slot_count, tile_rows, width)
    in_specs = [
        pl.BlockSpec((1, slot_count, tile_rows, width), lambda t, orb, m: (t, 0, 0, 0)),
        pl.BlockSpec((1, width, width), lambda t, orb, m: (t, 0, 0)),
    ]
    scratch = [pltpu.VMEM((slot_count, tile_rows, width), source.dtype)]
    operands = [orbitals, match, source, weights]
    if start is None:
        body = first_gamma_kernel
    else:
        body = next_gamma_kernel
        in_specs.append(pl.BlockSpec(memory_space=pl.ANY))
        scratch += [pltpu.VMEM(total_shape, jnp.float32), pltpu.SemaphoreType.DMA]
        operands.append(start)
    return pl.pallas_call(
        body,
        grid_spec=pltpu.PrefetchScalarGridSpec(
            num_scalar_prefetch=2,
            grid=(term_count,),
            in_specs=in_specs,
            out_specs=pl.BlockSpec(
                total_shape, lambda t, orb, m: (0, 0, 0, 0), pipeline_mode=pl.Buffered(1)
            ),
            scratch_shapes=scratch,
        ),
        out_shape=jax.ShapeDtypeStruct(total_shape, out_type),
        compiler_params=pltpu.CompilerParams(vmem_limit_bytes=56 << 20),
        cost_estimate=pl.CostEstimate(
            flops=2 * term_count * slot_count * tile_rows * width * width,
            bytes_accessed=2 * term_count * slot_count * tile_rows * width
            + 8 * orb_count * slot_count * tile_rows * width,
            transcendentals=0,
        ),
    )(*operands)


def exchange(blocks, axis):
    count = lax.axis_size(axis)
    me = lax.axis_index(axis)
    arrived = [lax.dynamic_index_in_dim(blocks, me, 0, keepdims=False)]
    for shift in range(1, count):
        block = lax.dynamic_index_in_dim(blocks, lax.rem(me + shift, count), 0, keepdims=False)
        arrived.append(lax.ppermute(block, axis, [(d, (d + shift) % count) for d in range(count)]))
    return arrived


def pair_weights(partial, energy_pair, vir_energy, counted):
    group_count = lax.axis_size("aux")
    share = lax.axis_index("aux")
    term_count, width = partial.shape[:2]
    share_terms = term_count // group_count
    parts = exchange(partial.reshape(group_count, share_terms, width, width), "aux")
    coulomb = parts[0].astype(jnp.float32)
    for part in parts[1:]:
        coulomb = coulomb + part.astype(jnp.float32)
    energy = lax.dynamic_slice_in_dim(energy_pair, share * share_terms, share_terms, 0)
    denominator = energy[:, None, None] - vir_energy[None, :, None] - vir_energy[None, None, :]
    amplitude = coulomb / denominator
    mixed = 2.0 * amplitude - jnp.swapaxes(amplitude, 1, 2)
    weights = lax.all_gather(mixed.astype(jnp.bfloat16), "aux", axis=0, tiled=True)
    if counted is None:
        return weights
    amplitude, mixed = amplitude[counted], mixed[counted]
    density = jnp.einsum(
        "rac,rbc->ab", amplitude, mixed, precision=lax.Precision.HIGHEST
    ) + jnp.einsum("rca,rcb->ab", amplitude, mixed, precision=lax.Precision.HIGHEST)
    return weights, density


def per_device(int_tiles, tile_ids, tile_counts, pair_list, occ_energy, vir_energy):
    peer_count = lax.axis_size("occ")
    group_count = lax.axis_size("aux")
    orb_count, slot_count, tile_rows, width = int_tiles.shape
    assert pair_list.shape[0] == peer_count and peer_count % 2 == 0
    half = peer_count // 2
    assert half % group_count == 0
    me = lax.axis_index("occ")

    slot_range = jnp.arange(slot_count, dtype=jnp.int32)
    live_ids = jnp.where(slot_range[None, :] < tile_counts, tile_ids, -1)
    packed = jnp.concatenate([pair_list.reshape(-1), live_ids.reshape(-1)])
    everyone = lax.all_gather(packed, "occ")
    everyone, own_tiles = lax.optimization_barrier((everyone, int_tiles))
    all_pairs = everyone[:, : 2 * peer_count].reshape(peer_count, peer_count, 2)
    all_ids = everyone[:, 2 * peer_count :].reshape(peer_count * orb_count, slot_count)

    near = me // half * half + jnp.arange(half, dtype=jnp.int32)
    far = lax.rem(near + half, peer_count)
    partner = lax.rem(me + half, peer_count)

    def wanted_of(owner):
        return jnp.stack([all_pairs[owner, near, 0], all_pairs[near, owner, 1]], axis=1)

    def terms_of(peers):
        remote = jnp.stack([all_pairs[peers, me, 0], all_pairs[me, peers, 1]], axis=1)
        own = jnp.stack([all_pairs[peers, me, 1], all_pairs[me, peers, 0]], axis=1)
        remote = peers[:, None] * orb_count + remote
        match = slot_match(live_ids[own.reshape(-1)], all_ids[remote.reshape(-1)])
        energy_pair = occ_energy[remote] + occ_energy[me * orb_count + own]
        return own, match.reshape(half, 2, slot_count), energy_pair

    groups = [list(range(half)), list(range(half, peer_count))]

    def near_exchange(tiles):
        return lax.all_to_all(
            tiles, "occ", split_axis=0, concat_axis=0, axis_index_groups=groups, tiled=True
        )

    swapped = [(d, (d + half) % peer_count) for d in range(peer_count)]
    partner_tiles = lax.ppermute(own_tiles, "occ", swapped)
    near_tiles = near_exchange(own_tiles[wanted_of(me).reshape(-1)])
    flipped = int_tiles.reshape(orb_count, slot_count * tile_rows, width).swapaxes(1, 2)

    own, match, energy_pair = terms_of(near)
    own, match = own.reshape(-1), match.reshape(-1, slot_count)
    partial = coulomb_call(own, match, near_tiles, flipped)
    partner_tiles, partial = lax.optimization_barrier((partner_tiles, partial))

    wanted = wanted_of(partner)
    first_tiles = near_exchange(partner_tiles[wanted[:, 0]])
    first_tiles, second_tiles = lax.optimization_barrier((first_tiles, partner_tiles[wanted[:, 1]]))
    second_tiles = near_exchange(second_tiles)

    weights, density = pair_weights(
        partial, energy_pair.reshape(-1), vir_energy, slice(None, None, 2)
    )
    gamma = gamma_call(own, match, near_tiles, weights, None, orb_count, jnp.float32)

    own, match, energy_pair = terms_of(far)
    partial = coulomb_call(own[:, 0], match[:, 0], first_tiles, flipped)
    weights, more_density = pair_weights(partial, energy_pair[:, 0], vir_energy, slice(None))
    gamma = gamma_call(own[:, 0], match[:, 0], first_tiles, weights, gamma, orb_count, jnp.float32)

    density = (density + more_density).astype(jnp.bfloat16)
    parts = exchange(density.reshape(group_count, width // group_count, width), "aux")
    density = parts[0].astype(jnp.float32)
    for part in parts[1:]:
        density = density + part.astype(jnp.float32)
    block = density.astype(jnp.bfloat16)
    for shift in range(1, half):
        turned = [(d, d // half * half + (d + shift) % half) for d in range(peer_count)]
        density = density + lax.ppermute(block, "occ", turned).astype(jnp.float32)

    second_tiles, gamma = lax.optimization_barrier((second_tiles, gamma))
    partial = coulomb_call(own[:, 1], match[:, 1], second_tiles, flipped)
    weights = pair_weights(partial, energy_pair[:, 1], vir_energy, None)
    weights, density = lax.optimization_barrier((weights, density))
    density = density + lax.ppermute(density.astype(jnp.bfloat16), "occ", swapped).astype(jnp.float32)
    gamma = gamma_call(own[:, 1], match[:, 1], second_tiles, weights, gamma, orb_count, jnp.bfloat16)
    return gamma, density


def solution(mesh):
    placed = (
        P("occ", "aux", None, None),
        P("occ", "aux"),
        P("occ", "aux"),
        P("occ", None),
        P(),
        P(),
    )
    return jax.shard_map(
        per_device,
        mesh=mesh,
        in_specs=placed,
        out_specs=(P("occ", "aux", None, None), P("aux", None)),
        check_vma=False,
    )
```

```python
import functools
import jax
import jax.numpy as jnp
from jax import lax
from jax.experimental import pallas as pl
from jax.experimental.pallas import tpu as pltpu
from jax.sharding import PartitionSpec as P

CHUNK_TILES = 4


def slot_match(wanted_ids, source_ids):
    same = (wanted_ids[:, :, None] == source_ids[:, None, :]) & (wanted_ids[:, :, None] >= 0)
    slots = jnp.arange(source_ids.shape[1], dtype=jnp.int32)
    return jnp.max(jnp.where(same, slots[None, None, :], -1), axis=2).astype(jnp.int32)


def gather_tiles(match_ref, row, source_ref, rows_ref):
    slot_count = source_ref.shape[1]
    for slot in range(slot_count):
        found = match_ref[row, slot]

        @pl.when(found >= 0)
        def _():
            rows_ref[slot] = source_ref[0, found]

        @pl.when(found < 0)
        def _():
            rows_ref[slot] = jnp.zeros(rows_ref.shape[1:], rows_ref.dtype)


def coulomb_kernel(orb_ref, match_ref, remote_ref, flipped_ref, out_ref, rows_ref):
    slot_count, tile_rows, width = rows_ref.shape
    gather_tiles(match_ref, pl.program_id(0), remote_ref, rows_ref)
    out_ref[0] = jnp.dot(
        flipped_ref[0],
        rows_ref[...].reshape(slot_count * tile_rows, width),
        preferred_element_type=jnp.float32,
    ).astype(out_ref.dtype)


def coulomb_call(orbitals, match, remote, flipped):
    term_count, slot_count, tile_rows, width = remote.shape
    return pl.pallas_call(
        coulomb_kernel,
        grid_spec=pltpu.PrefetchScalarGridSpec(
            num_scalar_prefetch=2,
            grid=(term_count,),
            in_specs=[
                pl.BlockSpec((1, slot_count, tile_rows, width), lambda t, orb, m: (t, 0, 0, 0)),
                pl.BlockSpec((1, width, slot_count * tile_rows), lambda t, orb, m: (orb[t], 0, 0)),
            ],
            out_specs=pl.BlockSpec((1, width, width), lambda t, orb, m: (t, 0, 0)),
            scratch_shapes=[pltpu.VMEM((slot_count, tile_rows, width), remote.dtype)],
        ),
        out_shape=jax.ShapeDtypeStruct((term_count, width, width), jnp.bfloat16),
        compiler_params=pltpu.CompilerParams(vmem_limit_bytes=56 << 20),
        cost_estimate=pl.CostEstimate(
            flops=2 * term_count * slot_count * tile_rows * width * width,
            bytes_accessed=4 * term_count * slot_count * tile_rows * width,
            transcendentals=0,
        ),
    )(orbitals, match, remote, flipped)


def add_terms(orb_ref, match_ref, source_ref, weight_ref, total_ref, rows_ref):
    term = pl.program_id(0)
    slot_count, tile_rows, width = rows_ref.shape
    gather_tiles(match_ref, term, source_ref, rows_ref)
    chunk = min(CHUNK_TILES, slot_count)
    orb = orb_ref[term]

    @pl.loop(0, slot_count // chunk)
    def _(step):
        first = step * chunk
        rows = rows_ref[pl.ds(first, chunk)].reshape(chunk * tile_rows, width)
        product = lax.dot_general(
            rows,
            weight_ref[0],
            (((1,), (1,)), ((), ())),
            preferred_element_type=jnp.float32,
        )
        total_ref[orb, pl.ds(first, chunk)] += product.reshape(chunk, tile_rows, width)


def first_gamma_kernel(
    counts, orb_ref, match_ref, near_ref, near_weight, far_ref, far_weight, total_ref, rows_ref
):
    @pl.when(pl.program_id(0) == 0)
    def _():
        total_ref[...] = jnp.zeros_like(total_ref)

    @pl.when(pl.program_id(0) < counts)
    def _():
        add_terms(orb_ref, match_ref, near_ref, near_weight, total_ref, rows_ref)

    @pl.when(pl.program_id(0) >= counts)
    def _():
        add_terms(orb_ref, match_ref, far_ref, far_weight, total_ref, rows_ref)


def next_gamma_kernel(
    orb_ref, match_ref, source_ref, weight_ref, start_ref, out_ref, rows_ref, total_ref, sem
):
    @pl.when(pl.program_id(0) == 0)
    def _():
        load = pltpu.make_async_copy(start_ref, total_ref, sem)
        load.start()
        load.wait()

    add_terms(orb_ref, match_ref, source_ref, weight_ref, total_ref, rows_ref)

    @pl.when(pl.program_id(0) == pl.num_programs(0) - 1)
    def _():
        out_ref[...] = total_ref[...].astype(out_ref.dtype)


def gamma_call(orbitals, match, sources, start, orb_count, out_type):
    slot_count, tile_rows, width = sources[0][0].shape[1:]
    total_shape = (orb_count, slot_count, tile_rows, width)
    in_specs, operands, first = [], [orbitals, match], 0
    for tiles, weights in sources:
        last = tiles.shape[0] - 1

        def place(t, first=first, last=last):
            return jnp.clip(t - first, 0, last)

        in_specs += [
            pl.BlockSpec(
                (1, slot_count, tile_rows, width),
                lambda t, orb, m, place=place: (place(t), 0, 0, 0),
            ),
            pl.BlockSpec((1, width, width), lambda t, orb, m, place=place: (place(t), 0, 0)),
        ]
        operands += [tiles, weights]
        first += tiles.shape[0]
    scratch = [pltpu.VMEM((slot_count, tile_rows, width), sources[0][0].dtype)]
    if start is None:
        body = functools.partial(first_gamma_kernel, sources[0][0].shape[0])
    else:
        body = next_gamma_kernel
        in_specs.append(pl.BlockSpec(memory_space=pl.ANY))
        scratch += [pltpu.VMEM(total_shape, jnp.float32), pltpu.SemaphoreType.DMA]
        operands.append(start)
    return pl.pallas_call(
        body,
        grid_spec=pltpu.PrefetchScalarGridSpec(
            num_scalar_prefetch=2,
            grid=(first,),
            in_specs=in_specs,
            out_specs=pl.BlockSpec(
                total_shape, lambda t, orb, m: (0, 0, 0, 0), pipeline_mode=pl.Buffered(1)
            ),
            scratch_shapes=scratch,
        ),
        out_shape=jax.ShapeDtypeStruct(total_shape, out_type),
        compiler_params=pltpu.CompilerParams(vmem_limit_bytes=56 << 20),
        cost_estimate=pl.CostEstimate(
            flops=2 * first * slot_count * tile_rows * width * width,
            bytes_accessed=2 * first * slot_count * tile_rows * width
            + 8 * orb_count * slot_count * tile_rows * width,
            transcendentals=0,
        ),
    )(*operands)


def exchange(blocks, axis):
    count = lax.axis_size(axis)
    me = lax.axis_index(axis)
    arrived = [lax.dynamic_index_in_dim(blocks, me, 0, keepdims=False)]
    for shift in range(1, count):
        block = lax.dynamic_index_in_dim(blocks, lax.rem(me + shift, count), 0, keepdims=False)
        arrived.append(lax.ppermute(block, axis, [(d, (d + shift) % count) for d in range(count)]))
    return arrived


def pair_weights(partial, energy_pair, vir_energy, counted):
    group_count = lax.axis_size("aux")
    share = lax.axis_index("aux")
    term_count, width = partial.shape[:2]
    share_terms = term_count // group_count
    parts = exchange(partial.reshape(group_count, share_terms, width, width), "aux")
    coulomb = parts[0].astype(jnp.float32)
    for part in parts[1:]:
        coulomb = coulomb + part.astype(jnp.float32)
    energy = lax.dynamic_slice_in_dim(energy_pair, share * share_terms, share_terms, 0)
    denominator = energy[:, None, None] - vir_energy[None, :, None] - vir_energy[None, None, :]
    amplitude = coulomb / denominator
    mixed = 2.0 * amplitude - jnp.swapaxes(amplitude, 1, 2)
    weights = lax.all_gather(mixed.astype(jnp.bfloat16), "aux", axis=0, tiled=True)
    if counted is None:
        return weights
    amplitude, mixed = amplitude[counted], mixed[counted]
    density = jnp.einsum(
        "rac,rbc->ab", amplitude, mixed, precision=lax.Precision.HIGHEST
    ) + jnp.einsum("rca,rcb->ab", amplitude, mixed, precision=lax.Precision.HIGHEST)
    return weights, density


def per_device(int_tiles, tile_ids, tile_counts, pair_list, occ_energy, vir_energy):
    peer_count = lax.axis_size("occ")
    group_count = lax.axis_size("aux")
    orb_count, slot_count, tile_rows, width = int_tiles.shape
    assert pair_list.shape[0] == peer_count and peer_count % 2 == 0
    half = peer_count // 2
    assert half % group_count == 0
    me = lax.axis_index("occ")

    slot_range = jnp.arange(slot_count, dtype=jnp.int32)
    live_ids = jnp.where(slot_range[None, :] < tile_counts, tile_ids, -1)
    packed = jnp.concatenate([pair_list.reshape(-1), live_ids.reshape(-1)])
    everyone = lax.all_gather(packed, "occ")
    everyone, own_tiles = lax.optimization_barrier((everyone, int_tiles))
    all_pairs = everyone[:, : 2 * peer_count].reshape(peer_count, peer_count, 2)
    all_ids = everyone[:, 2 * peer_count :].reshape(peer_count * orb_count, slot_count)

    near = me // half * half + jnp.arange(half, dtype=jnp.int32)
    far = lax.rem(near + half, peer_count)
    partner = lax.rem(me + half, peer_count)

    def wanted_of(owner):
        return jnp.stack([all_pairs[owner, near, 0], all_pairs[near, owner, 1]], axis=1)

    def terms_of(peers):
        remote = jnp.stack([all_pairs[peers, me, 0], all_pairs[me, peers, 1]], axis=1)
        own = jnp.stack([all_pairs[peers, me, 1], all_pairs[me, peers, 0]], axis=1)
        remote = peers[:, None] * orb_count + remote
        match = slot_match(live_ids[own.reshape(-1)], all_ids[remote.reshape(-1)])
        energy_pair = occ_energy[remote] + occ_energy[me * orb_count + own]
        return own, match.reshape(half, 2, slot_count), energy_pair

    groups = [list(range(half)), list(range(half, peer_count))]

    def near_exchange(tiles):
        return lax.all_to_all(
            tiles, "occ", split_axis=0, concat_axis=0, axis_index_groups=groups, tiled=True
        )

    swapped = [(d, (d + half) % peer_count) for d in range(peer_count)]
    partner_tiles = lax.ppermute(own_tiles, "occ", swapped)
    flipped = own_tiles.reshape(orb_count, slot_count * tile_rows, width).swapaxes(1, 2)
    near_tiles = near_exchange(own_tiles[wanted_of(me).reshape(-1)])

    wanted = wanted_of(partner)
    first_tiles = near_exchange(partner_tiles[wanted[:, 0]])
    near_tiles, partner_tiles = lax.optimization_barrier((near_tiles, partner_tiles))
    near_own, near_match, energy_pair = terms_of(near)
    near_own, near_match = near_own.reshape(-1), near_match.reshape(-1, slot_count)
    partial = coulomb_call(near_own, near_match, near_tiles, flipped)
    near_weights, density = pair_weights(
        partial, energy_pair.reshape(-1), vir_energy, slice(None, None, 2)
    )

    second_tiles, first_tiles, near_weights, density = lax.optimization_barrier(
        (partner_tiles[wanted[:, 1]], first_tiles, near_weights, density)
    )
    second_tiles = near_exchange(second_tiles)
    own, match, energy_pair = terms_of(far)
    partial = coulomb_call(own[:, 0], match[:, 0], first_tiles, flipped)
    first_weights, more_density = pair_weights(partial, energy_pair[:, 0], vir_energy, slice(None))

    density = (density + more_density).astype(jnp.bfloat16)
    parts = exchange(density.reshape(group_count, width // group_count, width), "aux")
    density = parts[0].astype(jnp.float32)
    for part in parts[1:]:
        density = density + part.astype(jnp.float32)
    density = density + lax.ppermute(density.astype(jnp.bfloat16), "occ", swapped).astype(jnp.float32)
    block = density.astype(jnp.bfloat16)
    for shift in range(1, half):
        turned = [(d, d // half * half + (d + shift) % half) for d in range(peer_count)]
        density = density + lax.ppermute(block, "occ", turned).astype(jnp.float32)

    gamma = gamma_call(
        jnp.concatenate([near_own, own[:, 0]]),
        jnp.concatenate([near_match, match[:, 0]]),
        [(near_tiles, near_weights), (first_tiles, first_weights)],
        None,
        orb_count,
        jnp.float32,
    )
    second_tiles, gamma = lax.optimization_barrier((second_tiles, gamma))
    partial = coulomb_call(own[:, 1], match[:, 1], second_tiles, flipped)
    weights = pair_weights(partial, energy_pair[:, 1], vir_energy, None)
    gamma = gamma_call(
        own[:, 1], match[:, 1], [(second_tiles, weights)], gamma, orb_count, jnp.bfloat16
    )
    return gamma, density


def solution(mesh):
    placed = (
        P("occ", "aux", None, None),
        P("occ", "aux"),
        P("occ", "aux"),
        P("occ", None),
        P(),
        P(),
    )
    return jax.shard_map(
        per_device,
        mesh=mesh,
        in_specs=placed,
        out_specs=(P("occ", "aux", None, None), P("aux", None)),
        check_vma=False,
    )
```

```python
import jax
import jax.numpy as jnp
from jax import lax
from jax.experimental import pallas as pl
from jax.experimental.pallas import tpu as pltpu
from jax.sharding import PartitionSpec as P

CHUNK_TILES = 4


def slot_match(wanted_ids, source_ids):
    same = (wanted_ids[:, :, None] == source_ids[:, None, :]) & (wanted_ids[:, :, None] >= 0)
    slots = jnp.arange(source_ids.shape[1], dtype=jnp.int32)
    return jnp.max(jnp.where(same, slots[None, None, :], -1), axis=2).astype(jnp.int32)


def gather_tiles(match_ref, row, source_ref, rows_ref):
    slot_count = source_ref.shape[1]
    for slot in range(slot_count):
        found = match_ref[row, slot]

        @pl.when(found >= 0)
        def _():
            rows_ref[slot] = source_ref[0, found]

        @pl.when(found < 0)
        def _():
            rows_ref[slot] = jnp.zeros(rows_ref.shape[1:], rows_ref.dtype)


def coulomb_kernel(orb_ref, match_ref, left_ref, right_ref, out_ref, rows_ref, total_ref):
    pair = pl.program_id(0)
    slot_count, tile_rows, width = rows_ref.shape
    gather_tiles(match_ref, pair, right_ref, rows_ref)
    total_ref[...] = jnp.zeros_like(total_ref)
    chunk = min(CHUNK_TILES, slot_count)

    @pl.loop(0, slot_count // chunk)
    def _(step):
        first = step * chunk
        left = left_ref[0, pl.ds(first, chunk)].reshape(chunk * tile_rows, width)
        right = rows_ref[pl.ds(first, chunk)].reshape(chunk * tile_rows, width)
        total_ref[...] += lax.dot_general(
            left, right, (((0,), (0,)), ((), ())), preferred_element_type=jnp.float32
        )

    out_ref[0] = total_ref[...].astype(out_ref.dtype)


def coulomb_call(orbitals, match, left, own):
    pair_count, slot_count, tile_rows, width = left.shape
    block = (1, slot_count, tile_rows, width)
    return pl.pallas_call(
        coulomb_kernel,
        grid_spec=pltpu.PrefetchScalarGridSpec(
            num_scalar_prefetch=2,
            grid=(pair_count,),
            in_specs=[
                pl.BlockSpec(block, lambda p, orb, m: (p, 0, 0, 0)),
                pl.BlockSpec(block, lambda p, orb, m: (orb[p], 0, 0, 0)),
            ],
            out_specs=pl.BlockSpec((1, width, width), lambda p, orb, m: (p, 0, 0)),
            scratch_shapes=[
                pltpu.VMEM((slot_count, tile_rows, width), left.dtype),
                pltpu.VMEM((width, width), jnp.float32),
            ],
        ),
        out_shape=jax.ShapeDtypeStruct((pair_count, width, width), jnp.bfloat16),
        compiler_params=pltpu.CompilerParams(vmem_limit_bytes=56 << 20),
        cost_estimate=pl.CostEstimate(
            flops=2 * pair_count * slot_count * tile_rows * width * width,
            bytes_accessed=4 * pair_count * slot_count * tile_rows * width,
            transcendentals=0,
        ),
    )(orbitals, match, left, own)


def add_terms(orb_ref, match_ref, source_ref, weight_ref, total_ref, rows_ref):
    term = pl.program_id(0)
    slot_count, tile_rows, width = rows_ref.shape
    gather_tiles(match_ref, term, source_ref, rows_ref)
    chunk = min(CHUNK_TILES, slot_count)
    orb = orb_ref[term]

    @pl.loop(0, slot_count // chunk)
    def _(step):
        first = step * chunk
        rows = rows_ref[pl.ds(first, chunk)].reshape(chunk * tile_rows, width)
        product = lax.dot_general(
            rows,
            weight_ref[0],
            (((1,), (0,)), ((), ())),
            preferred_element_type=jnp.float32,
        )
        total_ref[orb, pl.ds(first, chunk)] += product.reshape(chunk, tile_rows, width)


def first_gamma_kernel(orb_ref, match_ref, source_ref, weight_ref, total_ref, rows_ref):
    @pl.when(pl.program_id(0) == 0)
    def _():
        total_ref[...] = jnp.zeros_like(total_ref)

    add_terms(orb_ref, match_ref, source_ref, weight_ref, total_ref, rows_ref)


def last_gamma_kernel(
    orb_ref, match_ref, source_ref, weight_ref, start_ref, out_ref, rows_ref, total_ref, sem
):
    @pl.when(pl.program_id(0) == 0)
    def _():
        load = pltpu.make_async_copy(start_ref, total_ref, sem)
        load.start()
        load.wait()

    add_terms(orb_ref, match_ref, source_ref, weight_ref, total_ref, rows_ref)

    @pl.when(pl.program_id(0) == pl.num_programs(0) - 1)
    def _():
        out_ref[...] = total_ref[...].astype(out_ref.dtype)


def gamma_call(orbitals, match, source, weights, start, orb_count):
    term_count, slot_count, tile_rows, width = source.shape
    total_shape = (orb_count, slot_count, tile_rows, width)
    whole = pl.BlockSpec(
        total_shape, lambda t, orb, m: (0, 0, 0, 0), pipeline_mode=pl.Buffered(1)
    )
    in_specs = [
        pl.BlockSpec((1, slot_count, tile_rows, width), lambda t, orb, m: (t, 0, 0, 0)),
        pl.BlockSpec((1, width, width), lambda t, orb, m: (t, 0, 0)),
    ]
    scratch = [pltpu.VMEM((slot_count, tile_rows, width), source.dtype)]
    operands = [orbitals, match, source, weights]
    if start is None:
        body, out_type = first_gamma_kernel, jnp.float32
    else:
        body, out_type = last_gamma_kernel, jnp.bfloat16
        in_specs.append(pl.BlockSpec(memory_space=pl.ANY))
        scratch += [pltpu.VMEM(total_shape, jnp.float32), pltpu.SemaphoreType.DMA]
        operands.append(start)
    return pl.pallas_call(
        body,
        grid_spec=pltpu.PrefetchScalarGridSpec(
            num_scalar_prefetch=2,
            grid=(term_count,),
            in_specs=in_specs,
            out_specs=whole,
            scratch_shapes=scratch,
        ),
        out_shape=jax.ShapeDtypeStruct(total_shape, out_type),
        compiler_params=pltpu.CompilerParams(vmem_limit_bytes=56 << 20),
        cost_estimate=pl.CostEstimate(
            flops=2 * term_count * slot_count * tile_rows * width * width,
            bytes_accessed=2 * term_count * slot_count * tile_rows * width
            + 8 * orb_count * slot_count * tile_rows * width,
            transcendentals=0,
        ),
    )(*operands)


def exchange(blocks, axis):
    count = lax.axis_size(axis)
    me = lax.axis_index(axis)
    arrived = [lax.dynamic_index_in_dim(blocks, me, 0, keepdims=False)]
    for shift in range(1, count):
        block = lax.dynamic_index_in_dim(blocks, lax.rem(me + shift, count), 0, keepdims=False)
        arrived.append(lax.ppermute(block, axis, [(d, (d + shift) % count) for d in range(count)]))
    return arrived


def pair_weights(partial, energy_pair, vir_energy):
    group_count = lax.axis_size("aux")
    share = lax.axis_index("aux")
    term_count, width = partial.shape[:2]
    share_terms = term_count // group_count
    parts = exchange(partial.reshape(group_count, share_terms, width, width), "aux")
    coulomb = parts[0].astype(jnp.float32)
    for part in parts[1:]:
        coulomb = coulomb + part.astype(jnp.float32)
    energy = lax.dynamic_slice_in_dim(energy_pair, share * share_terms, share_terms, 0)
    denominator = energy[:, None, None] - vir_energy[None, :, None] - vir_energy[None, None, :]
    amplitude = coulomb / denominator
    mixed = 2.0 * amplitude - jnp.swapaxes(amplitude, 1, 2)
    weights = lax.all_gather(mixed.astype(jnp.bfloat16), "aux", axis=0, tiled=True)
    amplitude, mixed = amplitude[0::2], mixed[0::2]
    density = jnp.einsum(
        "rac,rbc->ab", amplitude, mixed, precision=lax.Precision.HIGHEST
    ) + jnp.einsum("rca,rcb->ab", amplitude, mixed, precision=lax.Precision.HIGHEST)
    return weights, density


def per_device(int_tiles, tile_ids, tile_counts, pair_list, occ_energy, vir_energy):
    peer_count = lax.axis_size("occ")
    group_count = lax.axis_size("aux")
    orb_count, slot_count, tile_rows, width = int_tiles.shape
    assert pair_list.shape[0] == peer_count and peer_count % 2 == 0
    half = peer_count // 2
    assert (2 * half) % (2 * group_count) == 0
    me = lax.axis_index("occ")

    slot_range = jnp.arange(slot_count, dtype=jnp.int32)
    live_ids = jnp.where(slot_range[None, :] < tile_counts, tile_ids, -1)
    packed = jnp.concatenate([pair_list.reshape(-1), live_ids.reshape(-1)])
    everyone = lax.all_gather(packed, "occ")
    everyone, own_tiles = lax.optimization_barrier((everyone, int_tiles))
    all_pairs = everyone[:, : 2 * peer_count].reshape(peer_count, peer_count, 2)
    all_ids = everyone[:, 2 * peer_count :].reshape(peer_count * orb_count, slot_count)

    near = me // half * half + jnp.arange(half, dtype=jnp.int32)
    far = lax.rem(near + half, peer_count)
    partner = lax.rem(me + half, peer_count)

    def wanted_of(owner):
        return jnp.stack([all_pairs[owner, near, 0], all_pairs[near, owner, 1]], axis=1).reshape(-1)

    def terms_of(peers):
        remote = jnp.stack([all_pairs[peers, me, 0], all_pairs[me, peers, 1]], axis=1)
        own = jnp.stack([all_pairs[peers, me, 1], all_pairs[me, peers, 0]], axis=1).reshape(-1)
        remote = (peers[:, None] * orb_count + remote).reshape(-1)
        remote_ids, own_ids = all_ids[remote], live_ids[own]
        energy_pair = occ_energy[remote] + occ_energy[me * orb_count + own]
        return (
            own,
            slot_match(remote_ids, own_ids),
            slot_match(own_ids, remote_ids),
            energy_pair,
        )

    groups = [list(range(half)), list(range(half, peer_count))]

    def near_exchange(tiles, owner):
        return lax.all_to_all(
            tiles[wanted_of(owner)],
            "occ",
            split_axis=0,
            concat_axis=0,
            axis_index_groups=groups,
            tiled=True,
        )

    swapped = [(d, (d + half) % peer_count) for d in range(peer_count)]
    partner_tiles = lax.ppermute(own_tiles, "occ", swapped)
    near_tiles = near_exchange(own_tiles, me)
    far_tiles = near_exchange(partner_tiles, partner)

    own, coulomb_match, near_match, energy_pair = terms_of(near)
    partial = coulomb_call(own, coulomb_match, near_tiles, int_tiles)
    weights, density = pair_weights(partial, energy_pair, vir_energy)
    gamma = gamma_call(own, near_match, near_tiles, weights, None, orb_count)

    far_tiles, gamma = lax.optimization_barrier((far_tiles, gamma))
    own, coulomb_match, far_match, energy_pair = terms_of(far)
    partial = coulomb_call(own, coulomb_match, far_tiles, int_tiles)
    weights, more_density = pair_weights(partial, energy_pair, vir_energy)

    density = (density + more_density).astype(jnp.bfloat16)
    parts = exchange(density.reshape(group_count, width // group_count, width), "aux")
    density = parts[0].astype(jnp.float32)
    for part in parts[1:]:
        density = density + part.astype(jnp.float32)
    density = density + lax.ppermute(density.astype(jnp.bfloat16), "occ", swapped).astype(jnp.float32)
    block = density.astype(jnp.bfloat16)
    for shift in range(1, half):
        turned = [(d, d // half * half + (d + shift) % half) for d in range(peer_count)]
        density = density + lax.ppermute(block, "occ", turned).astype(jnp.float32)

    gamma = gamma_call(own, far_match, far_tiles, weights, gamma, orb_count)
    return gamma, density


def solution(mesh):
    placed = (
        P("occ", "aux", None, None),
        P("occ", "aux"),
        P("occ", "aux"),
        P("occ", None),
        P(),
        P(),
    )
    return jax.shard_map(
        per_device,
        mesh=mesh,
        in_specs=placed,
        out_specs=(P("occ", "aux", None, None), P("aux", None)),
        check_vma=False,
    )
```
